128 devices in a mesh: dev: 128 (over z, x, y, core).
Axes of the slice: x: 4, y: 4, z: 4, core: 2. Of those that a mesh axis runs over, the one named last changes fastest.
Arguments:
- grain_boxes: float32 [256, 64, 4096], P('dev'), may hold values from 0 to 1
- box_anchors: int32 [256, 3], P('dev'), may hold values from 0 to 127, as said below
- migrations: int32 [128, 2], P('dev'), may hold values from 0 to 1, as said below
Outputs:
- new_boxes: float32 [256, 64, 4096], P('dev')
The draws below stay inside these ranges and needn't reach their ends.
Inputs may be any that keep to these rules, and one draw needn't show every extreme that they name: `box_anchors`: box b belongs to device d = b // 2; its first coordinate is d - 1, d or d + 1 modulo 128; the other two coordinates are 0 to 3. `migrations`: the two entries of a row differ, so each device hands exactly one box to each neighbour and receives one from each.
All inputs are finite; a program needn't handle non-finite values.
Results may differ from the reference program's by a relative error of at most 0.0003.
Values sent between devices are 32-bit elements; how exact they have to be, the bound alone decides.
No kernel may reach another device: no remote copies, remote signals or barrier semaphores. Data moves between devices by JAX's collectives and lax.ppermute only.
A program may use at most 128 MiB of HBM per device.

```python
import jax
import jax.numpy as jnp
from jax import lax

BOX = 64
BOX_DEV = 2
SUBSTEPS = 4
HALF = 32
TILE_YZ = 128
NX = 4096
BOXES = 256
N_DEV = 128


def draw_box_anchors(key, part):
    folded_key = jax.random.fold_in(key, 11)
    subkeys = jax.random.split(folded_key, 4)
    devices = BOXES // BOX_DEV
    offsets = jax.random.randint(subkeys[0], (BOXES,), -1, 2)
    first_box = jax.random.randint(subkeys[1], (), 0, BOX_DEV)
    final_box = (devices - 1) * BOX_DEV + jax.random.randint(subkeys[2], (), 0, BOX_DEV)
    box_index = jnp.arange(BOXES, dtype=jnp.int32)
    offsets = jnp.where(box_index == first_box, -1, offsets)
    offsets = jnp.where(box_index == final_box, 1, offsets)
    tile_first = (box_index // BOX_DEV + offsets) % devices
    lateral = jax.random.randint(subkeys[3], (BOXES, 2), 0, 4)
    return jnp.concatenate([tile_first[:, None], lateral], axis=1).astype(jnp.int32)


def draw_migrations(key, part):
    folded_key = jax.random.fold_in(key, 23)
    subkeys = jax.random.split(folded_key, 4)
    devices = BOXES // BOX_DEV
    right_slot = jax.random.randint(subkeys[0], (devices,), 0, BOX_DEV)
    row_index = jnp.arange(devices, dtype=jnp.int32)
    high_row = jax.random.randint(subkeys[1], (), 0, devices)
    low_row = (high_row + jax.random.randint(subkeys[2], (), 1, devices)) % devices
    right_slot = jnp.where(row_index == high_row, BOX_DEV - 1, right_slot)
    right_slot = jnp.where(row_index == low_row, 0, right_slot)
    left_slot = (right_slot + jax.random.randint(subkeys[3], (devices,), 1, BOX_DEV)) % BOX_DEV
    return jnp.stack([right_slot, left_slot], axis=1).astype(jnp.int32)


def shard_levels(rng, extent, pieces, least, largest):
    def one(axis_at, shards_of):
        heights = jax.random.uniform(jax.random.fold_in(jax.random.fold_in(rng, 6), axis_at), (shards_of,), jnp.float32, least / len(pieces), largest / len(pieces))
        return jnp.repeat(jnp.exp(heights), extent[axis_at] // shards_of).reshape((-1,) + (1,) * (len(extent) - axis_at - 1))

    gain = one(*pieces[0])
    for cut in pieces[1:]:
        gain = gain * one(*cut)
    return gain


def setup_inputs(seed: int = 0) -> dict:
    streams_of = jax.random.split(jax.random.key(seed), 4)
    grain_boxes = jnp.clip(1.0 * jax.random.uniform(streams_of[0], (BOXES, BOX, BOX * BOX), jnp.float32) ** shard_levels(streams_of[0], (BOXES, BOX, BOX * BOX), ((0, 128),), -0.2, 0.2), 0.0, 1.0)
    box_anchors = draw_box_anchors(jax.random.fold_in(streams_of[3], 71), 0)
    migrations = draw_migrations(jax.random.fold_in(streams_of[3], 71), 0)
    return dict(grain_boxes=grain_boxes, box_anchors=box_anchors, migrations=migrations)


growth_rate = 1.0
quartic_rate = 1.0
coupling = 1.5
gradient_energy = 2.0
time_step = 0.02


def laplacian(order_field):
    padded = jnp.pad(order_field, 1)
    beside = padded[2:, 1:-1, 1:-1] + padded[:-2, 1:-1, 1:-1]
    beside = beside + padded[1:-1, 2:, 1:-1] + padded[1:-1, :-2, 1:-1]
    beside = beside + padded[1:-1, 1:-1, 2:] + padded[1:-1, 1:-1, :-2]
    return beside - 6.0 * order_field


def relax_steps(order_field, others):
    for substep in range(SUBSTEPS):
        driving = growth_rate * order_field - quartic_rate * order_field * order_field * order_field
        driving = driving - 2.0 * coupling * order_field * others + gradient_energy * laplacian(order_field)
        order_field = order_field + time_step * driving
    return order_field


def reference(grain_boxes, box_anchors, migrations):
    grain_cubes = grain_boxes.reshape(BOXES, BOX, BOX, BOX)

    def deposit(box_index, grid_field):
        cube_field = lax.dynamic_index_in_dim(grain_cubes, box_index, 0, keepdims=False)
        anchor = lax.dynamic_index_in_dim(box_anchors, box_index, 0, keepdims=False)
        square = cube_field * cube_field
        placed = jnp.pad(square, ((0, 0), (0, TILE_YZ - BOX), (0, TILE_YZ - BOX)))
        placed = jnp.roll(placed, (anchor[1] * HALF, anchor[2] * HALF), axis=(1, 2))
        row_start = (anchor[0] * HALF).astype(jnp.int32)
        current = lax.dynamic_slice_in_dim(grid_field, row_start, BOX, 0)
        return lax.dynamic_update_slice_in_dim(grid_field, current + placed, row_start, 0)

    grid_field = jnp.zeros((NX + HALF, TILE_YZ, TILE_YZ), jnp.float32)
    grid_field = lax.fori_loop(0, BOXES, deposit, grid_field)
    covered = grid_field[:NX].at[:HALF].add(grid_field[NX:])
    extended = jnp.concatenate([covered, covered[:HALF]], axis=0)

    def relax_one(box_pair):
        cube_field, anchor = box_pair
        row_start = (anchor[0] * HALF).astype(jnp.int32)
        window = lax.dynamic_slice_in_dim(extended, row_start, BOX, 0)
        window = jnp.roll(window, (-anchor[1] * HALF, -anchor[2] * HALF), axis=(1, 2))[:, :BOX, :BOX]
        others = window - cube_field * cube_field
        return relax_steps(cube_field, others).reshape(BOX, BOX * BOX)

    relaxed = lax.map(relax_one, (grain_cubes, box_anchors))
    grouped = relaxed.reshape(N_DEV, BOX_DEV, BOX, BOX * BOX)
    device_rows = jnp.arange(N_DEV, dtype=jnp.int32)
    rightward = jnp.roll(grouped[device_rows, migrations[:, 0]], 1, axis=0)
    leftward = jnp.roll(grouped[device_rows, migrations[:, 1]], -1, axis=0)
    grouped = grouped.at[device_rows, migrations[:, 0]].set(rightward)
    grouped = grouped.at[device_rows, migrations[:, 1]].set(leftward)
    return grouped.reshape(BOXES, BOX, BOX * BOX)
```

```python
import functools

import jax
import jax.numpy as jnp
from jax import lax
from jax.experimental import pallas as pl
from jax.experimental.pallas import tpu as pltpu
from jax.sharding import PartitionSpec as P

SUBSTEPS = 4

growth_rate = 1.0
quartic_rate = 1.0
coupling = 1.5
gradient_energy = 2.0
time_step = 0.02

HALF_BLOCKS = 128
PIECE = (HALF_BLOCKS, 8, 128)
TILE = (2, 64, 4, 8, 128)


def meta_int(ref, index):
    return ref[0, 0, index].astype(jnp.int32)


def box_meta(ref, slot, flip):
    offset = jnp.where(slot == 0, meta_int(ref, 0), meta_int(ref, 1))
    row = jnp.where(slot == 0, meta_int(ref, 2), meta_int(ref, 3)) & 3
    column = jnp.where(slot == 0, meta_int(ref, 4), meta_int(ref, 5)) & 3
    return jnp.where(flip == 1, -offset, offset), row, column


def deposit(tile_ref, piece_ref, base, row, column):
    lane = lax.broadcasted_iota(jnp.int32, (8, 128), 1)
    inside = ((lane - 32 * column) & 127) < 64
    shift = 32 * column
    shift_odd = (32 * column + 64) & 127

    def body(step, carry):
        for sub in range(2):
            m = step * 2 + sub
            place = (16 * row + m) & 63
            for it in range(4):
                value = piece_ref[base + it * 32 + m]
                value = value * value
                even = jnp.where(inside, pltpu.roll(value, shift, 1), 0.0)
                odd = jnp.where(inside, pltpu.roll(value, shift_odd, 1), 0.0)
                tile_ref[0, place, it] += even
                tile_ref[1, place, it] += odd
        return carry

    lax.fori_loop(0, 16, body, 0)


def extract(tile_ref, out_ref, row, column):
    lane = lax.broadcasted_iota(jnp.int32, (8, 128), 1)
    low = lane < 64
    shift = (128 - 32 * column) & 127
    shift_odd = (64 - 32 * column) & 127

    def body(step, carry):
        for sub in range(2):
            m = step * 2 + sub
            place = (16 * row + m) & 63
            for it in range(4):
                even = pltpu.roll(tile_ref[0, place, it], shift, 1)
                odd = pltpu.roll(tile_ref[1, place, it], shift_odd, 1)
                out_ref[it * 32 + m] = jnp.where(low, even, odd)
        return carry

    lax.fori_loop(0, 16, body, 0)


def deposit_if(cond, tile_ref, piece_ref, slot, row, column):
    @pl.when(cond)
    def _():
        deposit(tile_ref, piece_ref, slot * HALF_BLOCKS, row, column)


def clear(tile_ref):
    def body(place, carry):
        for par in range(2):
            for it in range(4):
                tile_ref[par, place, it] = jnp.zeros((8, 128), jnp.float32)
        return carry

    lax.fori_loop(0, 64, body, 0)


def local_kernel(mine_outer, mine_inner, sib_outer, sib_inner, mine_meta, sib_meta, tile_0, tile_1):
    flip = meta_int(mine_meta, 8)
    clear(tile_0)
    clear(tile_1)
    for slot in range(2):
        u, row, column = box_meta(mine_meta, slot, flip)
        deposit_if(u == 0, tile_0, mine_outer, slot, row, column)
        deposit_if(u == -1, tile_0, mine_inner, slot, row, column)
        deposit_if(u == 1, tile_1, mine_outer, slot, row, column)
        deposit_if(u == 0, tile_1, mine_inner, slot, row, column)
        u, row, column = box_meta(sib_meta, slot, flip)
        deposit_if(u == -1, tile_0, sib_inner, slot, row, column)
        deposit_if(u == 0, tile_1, sib_inner, slot, row, column)
        deposit_if(u == -1, tile_1, sib_outer, slot, row, column)


def heading_outer(ref, flip):
    return jnp.where(flip == 1, meta_int(ref, 7), meta_int(ref, 6)) & 1


def inner_kernel(part, out_outer, beyond, mine_meta, sib_meta, out_meta, beyond_meta,
                 to_next, to_next_far, window_out, window_sib, tile, sem):
    copy = pltpu.make_async_copy(part, tile, sem)
    copy.start()
    copy.wait()
    flip = meta_int(mine_meta, 8)
    for slot in range(2):
        u, row, column = box_meta(out_meta, slot, flip)
        deposit_if(u == 1, tile, out_outer, slot, row, column)
        u, row, column = box_meta(beyond_meta, slot, flip)
        deposit_if(u == -1, tile, beyond, slot, row, column)
    leaving = heading_outer(sib_meta, flip)
    _, row, column = box_meta(sib_meta, leaving, flip)
    extract(tile, to_next, row, column)
    _, row, column = box_meta(beyond_meta, heading_outer(beyond_meta, flip), flip)
    extract(tile, to_next_far, row, column)
    _, row, column = box_meta(out_meta, heading_outer(out_meta, flip), flip)
    extract(tile, window_out, row, column)
    _, row, column = box_meta(sib_meta, 1 - leaving, flip)
    extract(tile, window_sib, row, column)


def outer_kernel(part, out_outer, out_inner, far_inner, mine_meta, sib_meta, out_meta, far_meta,
                 to_next, to_sib, window_out, window_sib, tile, sem):
    copy = pltpu.make_async_copy(part, tile, sem)
    copy.start()
    copy.wait()
    flip = meta_int(mine_meta, 8)
    for slot in range(2):
        u, row, column = box_meta(out_meta, slot, flip)
        deposit_if(u == 0, tile, out_outer, slot, row, column)
        deposit_if(u == 1, tile, out_inner, slot, row, column)
        u, row, column = box_meta(far_meta, slot, flip)
        deposit_if(u == 1, tile, far_inner, slot, row, column)
    leaving = heading_outer(sib_meta, flip)
    _, row, column = box_meta(sib_meta, leaving, flip)
    extract(tile, to_next, row, column)
    _, row, column = box_meta(mine_meta, heading_outer(mine_meta, flip), flip)
    extract(tile, to_sib, row, column)
    _, row, column = box_meta(out_meta, heading_outer(out_meta, flip), flip)
    extract(tile, window_out, row, column)
    _, row, column = box_meta(sib_meta, 1 - leaving, flip)
    extract(tile, window_sib, row, column)


def substep(source, target, factor):
    shape = (8, 128)
    lane = lax.broadcasted_iota(jnp.int32, shape, 1)
    sublane = lax.broadcasted_iota(jnp.int32, shape, 0)
    low = lane < 64
    last_z = (lane & 63) == 63
    first_z = (lane & 63) == 0
    top = sublane == 7
    bottom = sublane == 0
    zero = jnp.zeros(shape, jnp.float32)

    def swapped(m):
        return [pltpu.roll(source[it * 32 + m], 64, 1) for it in range(8)]

    def body(m, carry):
        before, here = carry
        following = jnp.minimum(m + 1, 31)
        after = [jnp.where(m == 31, zero, value) for value in swapped(following)]
        cells = [source[it * 32 + m] for it in range(8)]
        ups = [pltpu.roll(value, 7, 0) for value in cells] + [zero]
        downs = [zero] + [pltpu.roll(value, 1, 0) for value in cells]
        for it in range(8):
            value = cells[it]
            beside = jnp.where(top, ups[it + 1], ups[it])
            beside += jnp.where(bottom, downs[it], downs[it + 1])
            beside += here[it] + jnp.where(low, before[it], after[it])
            beside += jnp.where(last_z, 0.0, pltpu.roll(value, 127, 1))
            beside += jnp.where(first_z, 0.0, pltpu.roll(value, 1, 1))
            rate = factor[it * 32 + m] - (time_step * quartic_rate) * (value * value)
            target[it * 32 + m] = value * rate + (time_step * gradient_energy) * beside
        return here, after

    lax.fori_loop(0, 32, body, ([zero] * 8, swapped(0)))


def relax_kernel(scalars, *refs, first):
    (half_0, half_1), windows, rest = refs[:2], refs[2:6], refs[6:]
    result, factor, ping, pong = rest[-4:]
    flip, u = scalars[1], scalars[2]
    base = 1.0 + time_step * (growth_rate - 6.0 * gradient_energy)
    scale = 2.0 * coupling * time_step

    for g, half in ((0, half_0), (1, half_1)):
        at = pl.multiple_of(jnp.where(flip == 1, 1 - g, g) * HALF_BLOCKS, HALF_BLOCKS)
        tile = first + u + g
        for index, window in enumerate(windows):
            @pl.when(tile == first - 1 + index)
            def _(window=window, half=half, at=at):
                def body(n, carry):
                    for sub in range(8):
                        value = half[n * 8 + sub]
                        ping[at + n * 8 + sub] = value
                        factor[at + n * 8 + sub] = base - scale * (window[n * 8 + sub] - value * value)
                    return carry

                lax.fori_loop(0, HALF_BLOCKS // 8, body, 0)

    substep(ping, pong, factor)
    substep(pong, ping, factor)
    substep(ping, pong, factor)
    substep(pong, result.at[0], factor)


def whole(shape):
    return pl.BlockSpec(shape, lambda *_: (0,) * len(shape))


def piece_of_message():
    return pl.BlockSpec((2 * HALF_BLOCKS, 8, 128), lambda *_: (0, 0, 0))


def meta_of_message():
    return pl.BlockSpec((1, 8, 128), lambda *_: (2 * HALF_BLOCKS, 0, 0), memory_space=pltpu.SMEM)


def on_device(grain_boxes, box_anchors, migrations):
    devices = lax.axis_size("dev")
    position = lax.axis_index("dev")
    parity = position % 2
    chips = devices // 2

    def pairs_of(even_step, odd_step):
        pairs = []
        for chip in range(chips):
            pairs.append((2 * chip, (2 * chip + even_step) % devices))
            pairs.append((2 * chip + 1, (2 * chip + 1 + odd_step) % devices))
        return pairs

    sibling, outward = pairs_of(1, -1), pairs_of(-1, 1)
    inward, inward_far = pairs_of(2, -2), pairs_of(3, -3)

    def send(value, pairs):
        return lax.ppermute(value, "dev", pairs)

    boxes = grain_boxes.reshape(2, 8, 8, 32, 128).transpose(0, 1, 3, 2, 4)
    offsets = (box_anchors[:, 0] - position + 1) % devices - 1
    meta = jnp.concatenate(
        [offsets, box_anchors[:, 1], box_anchors[:, 2], migrations[0], parity[None]]
    ).astype(jnp.float32)
    meta = jnp.pad(meta.reshape(1, 1, 9), ((0, 0), (0, 7), (0, 119)))

    def message(start):
        part = lax.dynamic_slice_in_dim(boxes, start, 4, 1)
        return jnp.concatenate([part.reshape(2 * HALF_BLOCKS, 8, 128), meta])

    outer = message(parity * 4)
    inner = message(4 - parity * 4)

    out_outer = send(outer, outward)
    out_inner = send(inner, outward)
    far_inner = send(inner, inward)
    sib_outer = send(outer, sibling)
    sib_inner = send(inner, sibling)
    beyond = send(out_outer, sibling)

    data, info = piece_of_message(), meta_of_message()
    tile_type = jax.ShapeDtypeStruct(TILE, jnp.float32)
    piece_type = jax.ShapeDtypeStruct(PIECE, jnp.float32)
    params = pltpu.CompilerParams(vmem_limit_bytes=48 << 20)
    part_0, part_1 = pl.pallas_call(
        local_kernel,
        grid=(1,),
        in_specs=[data] * 4 + [info] * 2,
        out_specs=[whole(TILE)] * 2,
        out_shape=[tile_type] * 2,
        compiler_params=params,
        name="local_tiles",
    )(outer, inner, sib_outer, sib_inner, outer, sib_outer)

    hbm = pl.BlockSpec(memory_space=pl.ANY)
    scratch = [pltpu.VMEM(TILE, jnp.float32), pltpu.SemaphoreType.DMA(())]
    to_next, to_next_far, window_out_1, window_sib_1 = pl.pallas_call(
        inner_kernel,
        grid=(1,),
        in_specs=[hbm] + [data] * 2 + [info] * 4,
        out_specs=[whole(PIECE)] * 4,
        out_shape=[piece_type] * 4,
        scratch_shapes=scratch,
        compiler_params=params,
        name="inner_tile",
    )(part_1, out_outer, beyond, outer, sib_outer, out_outer, beyond)
    near_out = send(to_next, inward)
    near_sib = send(to_next_far, inward_far)

    to_next, to_sib, window_out_0, window_sib_0 = pl.pallas_call(
        outer_kernel,
        grid=(1,),
        in_specs=[hbm] + [data] * 3 + [info] * 4,
        out_specs=[whole(PIECE)] * 4,
        out_shape=[piece_type] * 4,
        scratch_shapes=scratch,
        compiler_params=params,
        name="outer_tile",
    )(part_0, out_outer, out_inner, far_inner, outer, sib_outer, out_outer, far_inner)
    far_out = send(to_next, inward)
    from_sib = send(to_sib, sibling)

    def numbers(message_meta, sign_slot, own_slot):
        values = message_meta[0, 0, :9].astype(jnp.int32)
        slot = values[sign_slot]
        offset = values[slot]
        return jnp.stack([slot, parity, jnp.where(parity == 1, -offset, offset), own_slot])

    box_type = jax.ShapeDtypeStruct((2, 2 * HALF_BLOCKS, 8, 128), jnp.float32)
    half = pl.BlockSpec(PIECE, lambda _, s: (s[0], 0, 0))
    box_out = pl.BlockSpec((1, 2 * HALF_BLOCKS, 8, 128), lambda _, s: (s[3], 0, 0, 0))
    box_scratch = [pltpu.VMEM((2 * HALF_BLOCKS, 8, 128), jnp.float32)] * 3

    def relax(name, first, scalars, halves, windows, held):
        return pl.pallas_call(
            functools.partial(relax_kernel, first=first),
            grid_spec=pltpu.PrefetchScalarGridSpec(
                num_scalar_prefetch=1,
                grid=(1,),
                in_specs=[half] * 2 + [whole(PIECE)] * 4 + [hbm] * len(held),
                out_specs=box_out,
                scratch_shapes=box_scratch,
            ),
            out_shape=box_type,
            input_output_aliases={7: 0} if held else {},
            compiler_params=params,
            name=name,
        )(scalars, *halves, *windows, *held)

    sib_scalars = numbers(sib_outer[2 * HALF_BLOCKS:], 7 - parity, migrations[0, 1 - parity])
    out_scalars = numbers(out_outer[2 * HALF_BLOCKS:], 6 + parity, migrations[0, parity])
    held = relax(
        "relax_sibling", 1, sib_scalars, (sib_inner, sib_outer),
        (window_sib_0, window_sib_1, from_sib, near_sib), (),
    )
    relaxed = relax(
        "relax_outer", -1, out_scalars, (out_inner, out_outer),
        (far_out, near_out, window_out_0, window_out_1), (held,),
    )
    return relaxed.reshape(2, 8, 32, 8, 128).transpose(0, 1, 3, 2, 4).reshape(2, 64, 4096)


def solution(mesh):
    in_specs = (P("dev", None, None), P("dev", None), P("dev", None))
    out_specs = P("dev", None, None)
    return jax.shard_map(
        on_device, mesh=mesh, in_specs=in_specs, out_specs=out_specs, check_vma=False
    )
```

```python
import functools

import jax
import jax.numpy as jnp
from jax import lax
from jax.experimental import pallas as pl
from jax.experimental.pallas import tpu as pltpu
from jax.sharding import PartitionSpec as P

SUBSTEPS = 4

growth_rate = 1.0
quartic_rate = 1.0
coupling = 1.5
gradient_energy = 2.0
time_step = 0.02

HALF_BLOCKS = 128
PIECE = (HALF_BLOCKS, 8, 128)
TILE = (2, 64, 4, 8, 128)


META = 2 * HALF_BLOCKS
BOX_BLOCKS = (8, 32, 8, 128)
PADDED = (34, 80, 128)


def load_metas(refs, metas, sems, at=META):
    copies = [
        pltpu.make_async_copy(ref.at[META if n else at], metas.at[n], sems.at[n]) for n, ref in enumerate(refs)
    ]
    for copy in copies:
        copy.start()
    for copy in copies:
        copy.wait()


def number(metas, who, index):
    return metas[who, 0, index].astype(jnp.int32)


def box_meta(metas, who, slot, flip):
    first = slot == 0
    offset = jnp.where(first, number(metas, who, 0), number(metas, who, 1))
    row = jnp.where(first, number(metas, who, 2), number(metas, who, 3)) & 3
    column = jnp.where(first, number(metas, who, 4), number(metas, who, 5)) & 3
    return jnp.where(flip == 1, -offset, offset), row, column


def inbound(metas, who, flip):
    return jnp.where(flip == 1, number(metas, who, 7), number(metas, who, 6)) & 1


def deposit(tile_ref, piece_ref, base, row, column):
    lane = lax.broadcasted_iota(jnp.int32, (8, 128), 1)
    inside = ((lane - 32 * column) & 127) < 64
    shift = 32 * column
    shift_odd = (32 * column + 64) & 127

    def body(step, carry):
        for sub in range(4):
            m = step * 4 + sub
            place = (16 * row + m) & 63
            for it in range(4):
                value = piece_ref[base + it * 32 + m]
                value = value * value
                even = jnp.where(inside, pltpu.roll(value, shift, 1), 0.0)
                odd = jnp.where(inside, pltpu.roll(value, shift_odd, 1), 0.0)
                tile_ref[0, place, it] += even
                tile_ref[1, place, it] += odd
        return carry

    lax.fori_loop(0, 8, body, 0)


def extract(tile_ref, out_ref, row, column):
    lane = lax.broadcasted_iota(jnp.int32, (8, 128), 1)
    low = lane < 64
    shift = (128 - 32 * column) & 127
    shift_odd = (192 - 32 * column) & 127

    def body(step, carry):
        for sub in range(4):
            m = step * 4 + sub
            place = (16 * row + m) & 63
            for it in range(4):
                even = pltpu.roll(tile_ref[0, place, it], shift, 1)
                odd = pltpu.roll(tile_ref[1, place, it], shift_odd, 1)
                out_ref[it * 32 + m] = jnp.where(low, even, odd)
        return carry

    lax.fori_loop(0, 8, body, 0)


def deposit_if(cond, tile_ref, piece_ref, slot, row, column):
    @pl.when(cond)
    def _():
        deposit(tile_ref, piece_ref, slot * HALF_BLOCKS, row, column)


def clear(tile_ref):
    def body(step, carry):
        for sub in range(4):
            for par in range(2):
                for it in range(4):
                    tile_ref[par, step * 4 + sub, it] = jnp.zeros((8, 128), jnp.float32)
        return carry

    lax.fori_loop(0, 16, body, 0)


def message_kernel(boxes, anchors_hbm, migrations_hbm, outer, inner, anchors, migrations, sem):
    position = lax.axis_index("dev")
    devices = lax.axis_size("dev")
    flip = position & 1
    small = [
        pltpu.make_async_copy(anchors_hbm, anchors, sem.at[16]),
        pltpu.make_async_copy(migrations_hbm, migrations, sem.at[17]),
    ]
    copies = []
    for message, first in ((outer, 4 * flip), (inner, 4 - 4 * flip)):
        for box in range(2):
            for it in range(4):
                at = pl.ds(box * HALF_BLOCKS + it * 32, 32)
                copies.append(
                    pltpu.make_async_copy(boxes.at[box, first + it], message.at[at], sem.at[len(copies)])
                )
    for copy in small + copies:
        copy.start()
    for copy in small:
        copy.wait()
    lane = lax.broadcasted_iota(jnp.int32, (8, 128), 1)
    values = []
    for box in range(2):
        ahead = anchors[box, 0] - position + 1
        ahead = jnp.where(ahead < 0, ahead + devices, ahead)
        values.append(jnp.where(ahead >= devices, ahead - devices, ahead) - 1)
    values += [anchors[box, axis] for axis in (1, 2) for box in range(2)]
    values += [migrations[0, 0], migrations[0, 1]]
    block = jnp.zeros((8, 128), jnp.int32)
    for index, value in enumerate(values):
        block = jnp.where(lane == index, value, block)
    block = block.astype(jnp.float32)
    outer[META] = block
    inner[META] = block
    for copy in copies:
        copy.wait()


def local_kernel(mine_outer, mine_inner, sib_outer, sib_inner, tile_0, tile_1, metas, sems):
    load_metas((mine_outer, sib_outer), metas, sems)
    flip = lax.axis_index("dev") & 1
    clear(tile_0)
    clear(tile_1)
    for slot in range(2):
        u, row, column = box_meta(metas, 0, slot, flip)
        deposit_if(u == 0, tile_0, mine_outer, slot, row, column)
        deposit_if(u == -1, tile_0, mine_inner, slot, row, column)
        deposit_if(u == 1, tile_1, mine_outer, slot, row, column)
        deposit_if(u == 0, tile_1, mine_inner, slot, row, column)
        u, row, column = box_meta(metas, 1, slot, flip)
        deposit_if(u == -1, tile_0, sib_inner, slot, row, column)
        deposit_if(u == 0, tile_1, sib_inner, slot, row, column)
        deposit_if(u == -1, tile_1, sib_outer, slot, row, column)


def inner_kernel(part, sib_outer, out_outer, beyond,
                 to_next, window_out, window_sib, tile, metas, sems):
    copy = pltpu.make_async_copy(part, tile, sems.at[3])
    copy.start()
    load_metas((sib_outer, out_outer, beyond), metas, sems)
    copy.wait()
    flip = lax.axis_index("dev") & 1
    for slot in range(2):
        u, row, column = box_meta(metas, 1, slot, flip)
        deposit_if(u == 1, tile, out_outer, slot, row, column)
        u, row, column = box_meta(metas, 2, slot, flip)
        deposit_if(u == -1, tile, beyond, slot, row, column)
    leaving = inbound(metas, 0, flip)
    _, row, column = box_meta(metas, 0, leaving, flip)
    extract(tile, to_next.at[:HALF_BLOCKS], row, column)
    _, row, column = box_meta(metas, 2, inbound(metas, 2, flip), flip)
    extract(tile, to_next.at[HALF_BLOCKS:], row, column)
    _, row, column = box_meta(metas, 1, inbound(metas, 1, flip), flip)
    extract(tile, window_out, row, column)
    _, row, column = box_meta(metas, 0, 1 - leaving, flip)
    extract(tile, window_sib, row, column)


def outer_kernel(part, mine_outer, sib_outer, out_outer, out_inners,
                 to_next, to_sib, window_out, window_sib, tile, metas, sems):
    copy = pltpu.make_async_copy(part, tile, sems.at[4])
    copy.start()
    load_metas((out_inners, out_outer, sib_outer, mine_outer), metas, sems, 2 * META + 1)
    copy.wait()
    flip = lax.axis_index("dev") & 1
    for slot in range(2):
        u, row, column = box_meta(metas, 1, slot, flip)
        deposit_if(u == 0, tile, out_outer, slot, row, column)
        deposit_if(u == 1, tile, out_inners, slot, row, column)
        u, row, column = box_meta(metas, 0, slot, flip)

        @pl.when(u == 1)
        def _(slot=slot, row=row, column=column):
            deposit(tile, out_inners, META + 1 + slot * HALF_BLOCKS, row, column)

    leaving = inbound(metas, 2, flip)
    _, row, column = box_meta(metas, 2, leaving, flip)
    extract(tile, to_next, row, column)
    _, row, column = box_meta(metas, 3, inbound(metas, 3, flip), flip)
    extract(tile, to_sib, row, column)
    _, row, column = box_meta(metas, 1, inbound(metas, 1, flip), flip)
    extract(tile, window_out, row, column)
    _, row, column = box_meta(metas, 2, 1 - leaving, flip)
    extract(tile, window_sib, row, column)


def substep(source, factor, store, first, last, width):
    shape = (8, 128)
    lane = lax.broadcasted_iota(jnp.int32, shape, 1)
    low = lane < 64
    last_z = (lane & 63) == 63
    first_z = (lane & 63) == 0

    def body(step, carry):
        for sub in range(width):
            m = step * width + sub
            for it in range(8):
                row = 8 + 8 * it
                value = source[m + 1, row:row + 8]
                beside = source[m + 1, row + 1:row + 9] + source[m + 1, row - 1:row + 7]
                lines = jnp.where(low, source[m + 2, row:row + 8], source[m, row:row + 8])
                beside += pltpu.roll(value + lines, 64, 1)
                beside += jnp.where(last_z, 0.0, pltpu.roll(value, 127, 1))
                beside += jnp.where(first_z, 0.0, pltpu.roll(value, 1, 1))
                rate = factor[m, 8 * it:8 * it + 8] - (time_step * quartic_rate) * (value * value)
                store(m, it, value * rate + (time_step * gradient_energy) * beside)
        return carry

    lax.fori_loop(first // width, last // width, body, 0)


def relax_kernel(half_0, half_1, mine_outer, *refs, first):
    windows, result_hbm, (result, factor, ping, pong, metas, sems) = refs[:4], refs[-7], refs[-6:]
    load_metas((half_1, mine_outer), metas, sems)
    flip = lax.axis_index("dev") & 1
    slot = inbound(metas, 0, flip) if first < 0 else 1 - inbound(metas, 0, flip)
    own_slot = inbound(metas, 1, flip)
    own_slot = own_slot if first < 0 else 1 - own_slot
    u, _, _ = box_meta(metas, 0, slot, flip)
    base = 1.0 + time_step * (growth_rate - 6.0 * gradient_energy)
    scale = 2.0 * coupling * time_step

    for buffer in (ping, pong):
        for at in (0, 33):
            buffer[at] = jnp.zeros(PADDED[1:], jnp.float32)
        for m in range(1, 33):
            buffer[m, 0:8] = jnp.zeros((8, 128), jnp.float32)
            buffer[m, 72:80] = jnp.zeros((8, 128), jnp.float32)

    for g, half in ((0, half_0), (1, half_1)):
        at = jnp.where(flip == 1, 1 - g, g) * 32
        tile = first + u + g
        for index, window in enumerate(windows):
            @pl.when(tile == first - 1 + index)
            def _(window=window, half=half, at=at):
                def body(step, carry):
                    for sub in range(4):
                        m = step * 4 + sub
                        for it in range(4):
                            value = half[slot * HALF_BLOCKS + it * 32 + m]
                            rows = pl.multiple_of(at + 8 * it, 8)
                            ping[m + 1, pl.ds(pl.multiple_of(rows + 8, 8), 8)] = value
                            others = window[it * 32 + m] - value * value
                            factor[m, pl.ds(rows, 8)] = base - scale * others
                    return carry

                lax.fori_loop(0, 8, body, 0)

    def to(buffer):
        def store(m, it, value):
            buffer[m + 1, 8 + 8 * it:16 + 8 * it] = value

        return store

    def to_result(m, it, value):
        result[it, m] = value

    substep(ping, factor, to(pong), 0, 32, 8)
    substep(pong, factor, to(ping), 0, 32, 8)
    substep(ping, factor, to(pong), 0, 32, 8)
    copies = []
    for part in range(2):
        substep(pong, factor, to_result, 16 * part, 16 * part + 16, 8)
        lines = pl.ds(16 * part, 16)
        copy = pltpu.make_async_copy(
            result.at[:, lines], result_hbm.at[own_slot, :, lines], sems.at[2 + part]
        )
        copy.start()
        copies.append(copy)
    for copy in copies:
        copy.wait()


def on_device(grain_boxes, box_anchors, migrations):
    devices = lax.axis_size("dev")
    chips = devices // 2

    def pairs_of(even_step, odd_step):
        pairs = []
        for chip in range(chips):
            pairs.append((2 * chip, (2 * chip + even_step) % devices))
            pairs.append((2 * chip + 1, (2 * chip + 1 + odd_step) % devices))
        return pairs

    sibling, outward = pairs_of(1, -1), pairs_of(-1, 1)
    inward = pairs_of(2, -2)

    def send(value, pairs):
        return lax.ppermute(value, "dev", pairs)

    boxes = grain_boxes.reshape(2, 8, 8, 32, 128).transpose(0, 1, 3, 2, 4)

    vmem = pl.BlockSpec(memory_space=pltpu.VMEM)
    anywhere = pl.BlockSpec(memory_space=pl.ANY)
    params = pltpu.CompilerParams(vmem_limit_bytes=48 << 20)
    message_type = jax.ShapeDtypeStruct((2 * HALF_BLOCKS + 1, 8, 128), jnp.float32)
    tile_type = jax.ShapeDtypeStruct(TILE, jnp.float32)
    piece_type = jax.ShapeDtypeStruct(PIECE, jnp.float32)

    def metas(count, sems):
        return [pltpu.SMEM((count, 8, 128), jnp.float32), pltpu.SemaphoreType.DMA((sems,))]

    outer, inner = pl.pallas_call(
        message_kernel,
        in_specs=[pl.BlockSpec(memory_space=pltpu.HBM)] * 3,
        out_specs=[vmem] * 2,
        out_shape=[message_type] * 2,
        scratch_shapes=[
            pltpu.SMEM((2, 3), jnp.int32),
            pltpu.SMEM((1, 2), jnp.int32),
            pltpu.SemaphoreType.DMA((18,)),
        ],
        compiler_params=params,
        name="messages",
    )(*(pltpu.with_memory_space_constraint(a, pltpu.HBM) for a in (boxes, box_anchors, migrations)))

    out_outer = send(outer, outward)
    sib_outer = send(outer, sibling)
    sib_inner = send(inner, sibling)
    out_inners = send(jnp.concatenate([inner, sib_inner]), outward)

    part_0, part_1 = pl.pallas_call(
        local_kernel,
        in_specs=[vmem] * 4,
        out_specs=[vmem] * 2,
        out_shape=[tile_type] * 2,
        scratch_shapes=metas(2, 2),
        compiler_params=params,
        name="local_tiles",
    )(outer, inner, sib_outer, sib_inner)

    out_outer, part_1 = lax.optimization_barrier((out_outer, part_1))
    beyond = send(out_outer, sibling)

    tile_scratch = [pltpu.VMEM(TILE, jnp.float32)]
    to_next, window_out_1, window_sib_1 = pl.pallas_call(
        inner_kernel,
        in_specs=[anywhere] + [vmem] * 3,
        out_specs=[vmem] * 3,
        out_shape=[jax.ShapeDtypeStruct((META, 8, 128), jnp.float32)] + [piece_type] * 2,
        scratch_shapes=tile_scratch + metas(3, 4),
        compiler_params=params,
        name="inner_tile",
    )(part_1, sib_outer, out_outer, beyond)
    near = send(to_next, inward)

    part_0, window_out_1 = lax.optimization_barrier((part_0, window_out_1))
    to_next, to_sib, window_out_0, window_sib_0 = pl.pallas_call(
        outer_kernel,
        in_specs=[anywhere] + [vmem] * 4,
        out_specs=[vmem] * 4,
        out_shape=[piece_type] * 4,
        scratch_shapes=tile_scratch + metas(4, 5),
        compiler_params=params,
        name="outer_tile",
    )(part_0, outer, sib_outer, out_outer, out_inners)
    far_out = send(to_next, inward)
    from_sib = send(to_sib, sibling)
    near, window_out_0 = lax.optimization_barrier((near, window_out_0))
    near_sib = send(near[HALF_BLOCKS:], sibling)

    def relax(name, first, halves, windows, held):
        return pl.pallas_call(
            functools.partial(relax_kernel, first=first),
            in_specs=[vmem] * 7 + [anywhere] * len(held),
            out_specs=anywhere,
            out_shape=jax.ShapeDtypeStruct((2,) + BOX_BLOCKS, jnp.float32),
            scratch_shapes=[
                pltpu.VMEM(BOX_BLOCKS, jnp.float32),
                pltpu.VMEM((32, 64, 128), jnp.float32),
                pltpu.VMEM(PADDED, jnp.float32),
                pltpu.VMEM(PADDED, jnp.float32),
            ] + metas(2, 4),
            input_output_aliases={7: 0} if held else {},
            compiler_params=params,
            name=name,
        )(*halves, outer, *windows, *held)

    held = relax(
        "relax_sibling", 1, (sib_inner, sib_outer),
        (window_sib_0, window_sib_1, from_sib, near_sib), (),
    )
    relaxed = relax(
        "relax_outer", -1, (out_inners, out_outer),
        (far_out, near, window_out_0, window_out_1), (held,),
    )
    return relaxed.transpose(0, 1, 3, 2, 4).reshape(grain_boxes.shape)


def solution(mesh):
    in_specs = (P("dev", None, None), P("dev", None), P("dev", None))
    out_specs = P("dev", None, None)
    return jax.shard_map(
        on_device, mesh=mesh, in_specs=in_specs, out_specs=out_specs, check_vma=False
    )
```

```python
import functools

import jax
import jax.numpy as jnp
from jax import lax
from jax.experimental import pallas as pl
from jax.experimental.pallas import tpu as pltpu
from jax.sharding import PartitionSpec as P

SUBSTEPS = 4

growth_rate = 1.0
quartic_rate = 1.0
coupling = 1.5
gradient_energy = 2.0
time_step = 0.02

HALF_BLOCKS = 128
PIECE = (HALF_BLOCKS, 8, 128)
TILE = (2, 64, 4, 8, 128)


META = 2 * HALF_BLOCKS
BOX_BLOCKS = (8, 32, 8, 128)
PADDED = (34, 80, 128)


def load_metas(refs, metas, sems, at=META):
    copies = [
        pltpu.make_async_copy(ref.at[META if n else at], metas.at[n], sems.at[n]) for n, ref in enumerate(refs)
    ]
    for copy in copies:
        copy.start()
    for copy in copies:
        copy.wait()


def number(metas, who, index):
    return metas[who, 0, index].astype(jnp.int32)


def box_meta(metas, who, slot, flip):
    first = slot == 0
    offset = jnp.where(first, number(metas, who, 0), number(metas, who, 1))
    row = jnp.where(first, number(metas, who, 2), number(metas, who, 3)) & 3
    column = jnp.where(first, number(metas, who, 4), number(metas, who, 5)) & 3
    return jnp.where(flip == 1, -offset, offset), row, column


def inbound(metas, who, flip):
    return jnp.where(flip == 1, number(metas, who, 7), number(metas, who, 6)) & 1


def deposit(tile_ref, piece_ref, base, row, column):
    lane = lax.broadcasted_iota(jnp.int32, (8, 128), 1)
    inside = ((lane - 32 * column) & 127) < 64
    shift = 32 * column
    shift_odd = (32 * column + 64) & 127

    def body(step, carry):
        for sub in range(16):
            m = step * 16 + sub
            place = (16 * row + m) & 63
            for it in range(4):
                value = piece_ref[base + it * 32 + m]
                value = value * value
                even = jnp.where(inside, pltpu.roll(value, shift, 1), 0.0)
                odd = jnp.where(inside, pltpu.roll(value, shift_odd, 1), 0.0)
                tile_ref[0, place, it] += even
                tile_ref[1, place, it] += odd
        return carry

    lax.fori_loop(0, 2, body, 0)


def extract(tile_ref, out_refs, row, column):
    lane = lax.broadcasted_iota(jnp.int32, (8, 128), 1)
    low = lane < 64
    shift = (128 - 32 * column) & 127
    shift_odd = (192 - 32 * column) & 127

    def body(step, carry):
        for sub in range(16):
            m = step * 16 + sub
            place = (16 * row + m) & 63
            for it in range(4):
                even = pltpu.roll(tile_ref[0, place, it], shift, 1)
                odd = pltpu.roll(tile_ref[1, place, it], shift_odd, 1)
                each = 4 // len(out_refs)
                out_refs[it // each][it % each * 32 + m] = jnp.where(low, even, odd)
        return carry

    lax.fori_loop(0, 2, body, 0)


def deposit_if(cond, tile_ref, piece_ref, slot, row, column):
    @pl.when(cond)
    def _():
        deposit(tile_ref, piece_ref, slot * HALF_BLOCKS, row, column)


def clear(tile_ref):
    def body(step, carry):
        for sub in range(4):
            for par in range(2):
                for it in range(4):
                    tile_ref[par, step * 4 + sub, it] = jnp.zeros((8, 128), jnp.float32)
        return carry

    lax.fori_loop(0, 16, body, 0)


def message_kernel(boxes, anchors_hbm, migrations_hbm, outer, inner, anchors, migrations, sem):
    position = lax.axis_index("dev")
    devices = lax.axis_size("dev")
    flip = position & 1
    small = [
        pltpu.make_async_copy(anchors_hbm, anchors, sem.at[16]),
        pltpu.make_async_copy(migrations_hbm, migrations, sem.at[17]),
    ]
    copies = []
    for message, first in ((outer, 4 * flip), (inner, 4 - 4 * flip)):
        for box in range(2):
            for it in range(4):
                at = pl.ds(box * HALF_BLOCKS + it * 32, 32)
                copies.append(
                    pltpu.make_async_copy(boxes.at[box, first + it], message.at[at], sem.at[len(copies)])
                )
    for copy in small + copies:
        copy.start()
    for copy in small:
        copy.wait()
    lane = lax.broadcasted_iota(jnp.int32, (8, 128), 1)
    values = []
    for box in range(2):
        ahead = anchors[box, 0] - position + 1
        ahead = jnp.where(ahead < 0, ahead + devices, ahead)
        values.append(jnp.where(ahead >= devices, ahead - devices, ahead) - 1)
    values += [anchors[box, axis] for axis in (1, 2) for box in range(2)]
    values += [migrations[0, 0], migrations[0, 1]]
    block = jnp.zeros((8, 128), jnp.int32)
    for index, value in enumerate(values):
        block = jnp.where(lane == index, value, block)
    block = block.astype(jnp.float32)
    outer[META] = block
    inner[META] = block
    for copy in copies:
        copy.wait()


def local_kernel(mine_outer, mine_inner, sib_outer, sib_inner, tile_0, tile_1, metas, sems):
    load_metas((mine_outer, sib_outer), metas, sems)
    flip = lax.axis_index("dev") & 1
    clear(tile_0)
    clear(tile_1)
    for slot in range(2):
        u, row, column = box_meta(metas, 0, slot, flip)
        deposit_if(u == 0, tile_0, mine_outer, slot, row, column)
        deposit_if(u == -1, tile_0, mine_inner, slot, row, column)
        deposit_if(u == 1, tile_1, mine_outer, slot, row, column)
        deposit_if(u == 0, tile_1, mine_inner, slot, row, column)
        u, row, column = box_meta(metas, 1, slot, flip)
        deposit_if(u == -1, tile_0, sib_inner, slot, row, column)
        deposit_if(u == 0, tile_1, sib_inner, slot, row, column)
        deposit_if(u == -1, tile_1, sib_outer, slot, row, column)


def inner_kernel(part, sib_outer, out_outer, beyond,
                 to_next, cross_0, cross_1, window_out, window_sib, tile, metas, sems):
    copy = pltpu.make_async_copy(part, tile, sems.at[3])
    copy.start()
    load_metas((sib_outer, out_outer, beyond), metas, sems)
    copy.wait()
    flip = lax.axis_index("dev") & 1
    for slot in range(2):
        u, row, column = box_meta(metas, 1, slot, flip)
        deposit_if(u == 1, tile, out_outer, slot, row, column)
        u, row, column = box_meta(metas, 2, slot, flip)
        deposit_if(u == -1, tile, beyond, slot, row, column)
    leaving = inbound(metas, 0, flip)
    _, row, column = box_meta(metas, 0, leaving, flip)
    extract(tile, (to_next,), row, column)
    _, row, column = box_meta(metas, 2, inbound(metas, 2, flip), flip)
    extract(tile, (cross_0, cross_1), row, column)
    _, row, column = box_meta(metas, 1, inbound(metas, 1, flip), flip)
    extract(tile, (window_out,), row, column)
    _, row, column = box_meta(metas, 0, 1 - leaving, flip)
    extract(tile, (window_sib,), row, column)


def outer_kernel(part, mine_outer, sib_outer, out_outer, out_inners,
                 to_next, sib_0, sib_1, window_out, window_sib, tile, metas, sems):
    copy = pltpu.make_async_copy(part, tile, sems.at[4])
    copy.start()
    load_metas((out_inners, out_outer, sib_outer, mine_outer), metas, sems, 2 * META + 1)
    copy.wait()
    flip = lax.axis_index("dev") & 1
    for slot in range(2):
        u, row, column = box_meta(metas, 1, slot, flip)
        deposit_if(u == 0, tile, out_outer, slot, row, column)
        deposit_if(u == 1, tile, out_inners, slot, row, column)
        u, row, column = box_meta(metas, 0, slot, flip)

        @pl.when(u == 1)
        def _(slot=slot, row=row, column=column):
            deposit(tile, out_inners, META + 1 + slot * HALF_BLOCKS, row, column)

    leaving = inbound(metas, 2, flip)
    _, row, column = box_meta(metas, 2, leaving, flip)
    extract(tile, (to_next,), row, column)
    _, row, column = box_meta(metas, 3, inbound(metas, 3, flip), flip)
    extract(tile, (sib_0, sib_1), row, column)
    _, row, column = box_meta(metas, 1, inbound(metas, 1, flip), flip)
    extract(tile, (window_out,), row, column)
    _, row, column = box_meta(metas, 2, 1 - leaving, flip)
    extract(tile, (window_sib,), row, column)


def neighbour_table():
    source = lax.broadcasted_iota(jnp.int32, (256, 128), 0) & 127
    target = lax.broadcasted_iota(jnp.int32, (256, 128), 1)
    beside = (jnp.abs(source - target) == 1) & ((source >> 6) == (target >> 6))
    return jnp.where(beside, 1.0, 0.0).astype(jnp.bfloat16)


def substep(source, factor, target, table):
    low = lax.broadcasted_iota(jnp.int32, (8, 128), 1) < 64
    parts = []
    for m in range(32):
        line = source[m + 1, 8:72]
        upper = line.astype(jnp.bfloat16)
        lower = (line - upper.astype(jnp.float32)).astype(jnp.bfloat16)
        parts.append(jnp.concatenate([upper, lower], axis=1))
    along = jnp.dot(jnp.concatenate(parts), table, preferred_element_type=jnp.float32)
    for m in range(32):
        for it in range(8):
            row = 8 + 8 * it
            value = source[m + 1, row:row + 8]
            beside = source[m + 1, row + 1:row + 9] + source[m + 1, row - 1:row + 7]
            lines = jnp.where(low, source[m + 2, row:row + 8], source[m, row:row + 8])
            beside += pltpu.roll(value + lines, 64, 1) + along[64 * m + 8 * it:64 * m + 8 * it + 8]
            rate = factor[m, 8 * it:8 * it + 8] - (time_step * quartic_rate) * (value * value)
            target[m + 1, row:row + 8] = value * rate + (time_step * gradient_energy) * beside


def relax_kernel(half_0, half_1, mine_outer, *refs, first, sizes):
    result_hbm, (factor, ping, pong, metas, sems) = refs[-6], refs[-5:]
    windows, at = [], 0
    for size in sizes:
        windows.append(refs[at:at + size])
        at += size
    load_metas((half_1, mine_outer), metas, sems)
    flip = lax.axis_index("dev") & 1
    slot = inbound(metas, 0, flip) if first < 0 else 1 - inbound(metas, 0, flip)
    own_slot = inbound(metas, 1, flip)
    own_slot = own_slot if first < 0 else 1 - own_slot
    u, _, _ = box_meta(metas, 0, slot, flip)
    base = 1.0 + time_step * (growth_rate - 6.0 * gradient_energy)
    scale = 2.0 * coupling * time_step

    for buffer in (ping, pong):
        for at in (0, 33):
            buffer[at] = jnp.zeros(PADDED[1:], jnp.float32)
        for m in range(1, 33):
            buffer[m, 0:8] = jnp.zeros((8, 128), jnp.float32)
            buffer[m, 72:80] = jnp.zeros((8, 128), jnp.float32)

    for g, half in ((0, half_0), (1, half_1)):
        at = jnp.where(flip == 1, 1 - g, g) * 32
        tile = first + u + g
        for index, window in enumerate(windows):
            @pl.when(tile == first - 1 + index)
            def _(window=window, half=half, at=at):
                def body(step, carry):
                    for sub in range(8):
                        m = step * 8 + sub
                        for it in range(4):
                            value = half[slot * HALF_BLOCKS + it * 32 + m]
                            rows = pl.multiple_of(at + 8 * it, 8)
                            ping[m + 1, pl.ds(pl.multiple_of(rows + 8, 8), 8)] = value
                            each = 4 // len(window)
                            others = window[it // each][it % each * 32 + m] - value * value
                            factor[m, pl.ds(rows, 8)] = base - scale * others
                    return carry

                lax.fori_loop(0, 4, body, 0)

    table = neighbour_table()

    def twice(step, carry):
        substep(ping, factor, pong, table)
        substep(pong, factor, ping, table)
        return carry

    lax.fori_loop(0, SUBSTEPS // 2, twice, 0)
    copies = []
    for it in range(8):
        copies.append(pltpu.make_async_copy(
            ping.at[1:33, 8 + 8 * it:16 + 8 * it], result_hbm.at[own_slot, it], sems.at[2 + it]
        ))
    for copy in copies:
        copy.start()
    for copy in copies:
        copy.wait()


def on_device(grain_boxes, box_anchors, migrations):
    devices = lax.axis_size("dev")
    chips = devices // 2

    def pairs_of(even_step, odd_step):
        pairs = []
        for chip in range(chips):
            pairs.append((2 * chip, (2 * chip + even_step) % devices))
            pairs.append((2 * chip + 1, (2 * chip + 1 + odd_step) % devices))
        return pairs

    sibling, outward = pairs_of(1, -1), pairs_of(-1, 1)
    inward = pairs_of(2, -2)

    def send(value, pairs):
        return lax.ppermute(value, "dev", pairs)

    boxes = grain_boxes.reshape(2, 8, 8, 32, 128).transpose(0, 1, 3, 2, 4)

    vmem = pl.BlockSpec(memory_space=pltpu.VMEM)
    anywhere = pl.BlockSpec(memory_space=pl.ANY)
    params = pltpu.CompilerParams(vmem_limit_bytes=12 << 20)
    message_type = jax.ShapeDtypeStruct((2 * HALF_BLOCKS + 1, 8, 128), jnp.float32)
    tile_type = jax.ShapeDtypeStruct(TILE, jnp.float32)
    part_type = jax.ShapeDtypeStruct((HALF_BLOCKS // 2, 8, 128), jnp.float32)
    piece_type = jax.ShapeDtypeStruct(PIECE, jnp.float32)

    def metas(count, sems):
        return [pltpu.SMEM((count, 8, 128), jnp.float32), pltpu.SemaphoreType.DMA((sems,))]

    outer, inner = pl.pallas_call(
        message_kernel,
        in_specs=[pl.BlockSpec(memory_space=pltpu.HBM)] * 3,
        out_specs=[vmem] * 2,
        out_shape=[message_type] * 2,
        scratch_shapes=[
            pltpu.SMEM((2, 3), jnp.int32),
            pltpu.SMEM((1, 2), jnp.int32),
            pltpu.SemaphoreType.DMA((18,)),
        ],
        compiler_params=params,
        name="messages",
    )(*(pltpu.with_memory_space_constraint(a, pltpu.HBM) for a in (boxes, box_anchors, migrations)))

    out_outer = send(outer, outward)
    sib_outer = send(outer, sibling)
    sib_inner = send(inner, sibling)
    out_inners = send(jnp.concatenate([inner, sib_inner]), outward)

    part_0, part_1 = pl.pallas_call(
        local_kernel,
        in_specs=[vmem] * 4,
        out_specs=[vmem] * 2,
        out_shape=[tile_type] * 2,
        scratch_shapes=metas(2, 2),
        compiler_params=params,
        name="local_tiles",
    )(outer, inner, sib_outer, sib_inner)

    out_outer, part_1 = lax.optimization_barrier((out_outer, part_1))
    beyond = send(out_outer, sibling)

    tile_scratch = [pltpu.VMEM(TILE, jnp.float32)]
    to_next, cross_0, cross_1, window_out_1, window_sib_1 = pl.pallas_call(
        inner_kernel,
        in_specs=[anywhere] + [vmem] * 3,
        out_specs=[vmem] * 5,
        out_shape=[piece_type] + [part_type] * 2 + [piece_type] * 2,
        scratch_shapes=tile_scratch + metas(3, 4),
        compiler_params=params,
        name="inner_tile",
    )(part_1, sib_outer, out_outer, beyond)
    near = [send(value, inward) for value in (cross_0, cross_1, to_next)]

    part_0, window_out_1 = lax.optimization_barrier((part_0, window_out_1))
    to_next, to_sib_0, to_sib_1, window_out_0, window_sib_0 = pl.pallas_call(
        outer_kernel,
        in_specs=[anywhere] + [vmem] * 4,
        out_specs=[vmem] * 5,
        out_shape=[piece_type] + [part_type] * 2 + [piece_type] * 2,
        scratch_shapes=tile_scratch + metas(4, 5),
        compiler_params=params,
        name="outer_tile",
    )(part_0, outer, sib_outer, out_outer, out_inners)
    far_out = send(to_next, inward)
    from_sib = [send(value, sibling) for value in (to_sib_0, to_sib_1)]
    *near, window_out_0 = lax.optimization_barrier((*near, window_out_0))
    near_sib = [send(value, sibling) for value in near[:2]]

    def relax(name, first, halves, windows, held):
        flat = [value for window in windows for value in window]
        return pl.pallas_call(
            functools.partial(relax_kernel, first=first, sizes=[len(w) for w in windows]),
            in_specs=[vmem] * (3 + len(flat)) + [anywhere] * len(held),
            out_specs=anywhere,
            out_shape=jax.ShapeDtypeStruct((2,) + BOX_BLOCKS, jnp.float32),
            scratch_shapes=[
                pltpu.VMEM((32, 64, 128), jnp.float32),
                pltpu.VMEM(PADDED, jnp.float32),
                pltpu.VMEM(PADDED, jnp.float32),
            ] + metas(2, 10),
            input_output_aliases={3 + len(flat): 0} if held else {},
            compiler_params=params,
            name=name,
        )(*halves, outer, *flat, *held)

    held = relax(
        "relax_sibling", 1, (sib_inner, sib_outer),
        ([window_sib_0], [window_sib_1], from_sib, near_sib), (),
    )
    relaxed = relax(
        "relax_outer", -1, (out_inners, out_outer),
        ([far_out], near[2:], [window_out_0], [window_out_1]), (held,),
    )
    return relaxed.transpose(0, 1, 3, 2, 4).reshape(grain_boxes.shape)


def solution(mesh):
    in_specs = (P("dev", None, None), P("dev", None), P("dev", None))
    out_specs = P("dev", None, None)
    return jax.shard_map(
        on_device, mesh=mesh, in_specs=in_specs, out_specs=out_specs, check_vma=False
    )
```

```python
import functools

import jax
import jax.numpy as jnp
from jax import lax
from jax.experimental import pallas as pl
from jax.experimental.pallas import tpu as pltpu
from jax.sharding import PartitionSpec as P

SUBSTEPS = 4

growth_rate = 1.0
quartic_rate = 1.0
coupling = 1.5
gradient_energy = 2.0
time_step = 0.02

HALF_BLOCKS = 128
PIECE = (HALF_BLOCKS, 8, 128)
TILE = (2, 64, 4, 8, 128)


META = 2 * HALF_BLOCKS
BOX_BLOCKS = (8, 32, 8, 128)
PADDED = (34, 80, 128)


def load_metas(refs, metas, sems, at=META, meanwhile=None):
    copies = [
        pltpu.make_async_copy(ref.at[META if n else at], metas.at[n], sems.at[n]) for n, ref in enumerate(refs)
    ]
    for copy in copies:
        copy.start()
    if meanwhile is not None:
        meanwhile()
    for copy in copies:
        copy.wait()


def number(metas, who, index):
    return metas[who, 0, index].astype(jnp.int32)


def box_meta(metas, who, slot, flip):
    first = slot == 0
    offset = jnp.where(first, number(metas, who, 0), number(metas, who, 1))
    row = jnp.where(first, number(metas, who, 2), number(metas, who, 3)) & 3
    column = jnp.where(first, number(metas, who, 4), number(metas, who, 5)) & 3
    return jnp.where(flip == 1, -offset, offset), row, column


def inbound(metas, who, flip):
    return jnp.where(flip == 1, number(metas, who, 7), number(metas, who, 6)) & 1


def deposit(tile_ref, piece_ref, base, row, column):
    lane = lax.broadcasted_iota(jnp.int32, (8, 128), 1)
    inside = ((lane - 32 * column) & 127) < 64
    shift = 32 * column
    shift_odd = (32 * column + 64) & 127

    def body(step, carry):
        for sub in range(16):
            m = step * 16 + sub
            place = (16 * row + m) & 63
            for it in range(4):
                value = piece_ref[base + it * 32 + m]
                value = value * value
                even = jnp.where(inside, pltpu.roll(value, shift, 1), 0.0)
                odd = jnp.where(inside, pltpu.roll(value, shift_odd, 1), 0.0)
                tile_ref[0, place, it] += even
                tile_ref[1, place, it] += odd
        return carry

    lax.fori_loop(0, 2, body, 0)


def extract(tile_ref, out_refs, row, column):
    lane = lax.broadcasted_iota(jnp.int32, (8, 128), 1)
    low = lane < 64
    shift = (128 - 32 * column) & 127
    shift_odd = (192 - 32 * column) & 127

    def body(step, carry):
        for sub in range(16):
            m = step * 16 + sub
            place = (16 * row + m) & 63
            for it in range(4):
                even = pltpu.roll(tile_ref[0, place, it], shift, 1)
                odd = pltpu.roll(tile_ref[1, place, it], shift_odd, 1)
                each = 4 // len(out_refs)
                out_refs[it // each][it % each * 32 + m] = jnp.where(low, even, odd)
        return carry

    lax.fori_loop(0, 2, body, 0)


def deposit_if(cond, tile_ref, piece_ref, slot, row, column):
    @pl.when(cond)
    def _():
        deposit(tile_ref, piece_ref, slot * HALF_BLOCKS, row, column)


def clear(tile_ref):
    def body(step, carry):
        for sub in range(4):
            for par in range(2):
                for it in range(4):
                    tile_ref[par, step * 4 + sub, it] = jnp.zeros((8, 128), jnp.float32)
        return carry

    lax.fori_loop(0, 16, body, 0)


def message_kernel(boxes, anchors_hbm, migrations_hbm, outer, inner, anchors, migrations, sem):
    position = lax.axis_index("dev")
    devices = lax.axis_size("dev")
    flip = position & 1
    small = [
        pltpu.make_async_copy(anchors_hbm, anchors, sem.at[16]),
        pltpu.make_async_copy(migrations_hbm, migrations, sem.at[17]),
    ]
    copies = []
    for message, first in ((outer, 4 * flip), (inner, 4 - 4 * flip)):
        for box in range(2):
            for it in range(4):
                at = pl.ds(box * HALF_BLOCKS + it * 32, 32)
                copies.append(
                    pltpu.make_async_copy(boxes.at[box, first + it], message.at[at], sem.at[len(copies)])
                )
    for copy in small + copies:
        copy.start()
    for copy in small:
        copy.wait()
    lane = lax.broadcasted_iota(jnp.int32, (8, 128), 1)
    values = []
    for box in range(2):
        ahead = anchors[box, 0] - position + 1
        ahead = jnp.where(ahead < 0, ahead + devices, ahead)
        values.append(jnp.where(ahead >= devices, ahead - devices, ahead) - 1)
    values += [anchors[box, axis] for axis in (1, 2) for box in range(2)]
    values += [migrations[0, 0], migrations[0, 1]]
    block = jnp.zeros((8, 128), jnp.int32)
    for index, value in enumerate(values):
        block = jnp.where(lane == index, value, block)
    block = block.astype(jnp.float32)
    outer[META] = block
    inner[META] = block
    for copy in copies:
        copy.wait()


def local_kernel(mine_outer, mine_inner, sib_outer, sib_inner, tile_0, tile_1, metas, sems):
    load_metas((mine_outer, sib_outer), metas, sems)
    flip = lax.axis_index("dev") & 1
    clear(tile_0)
    clear(tile_1)
    for slot in range(2):
        u, row, column = box_meta(metas, 0, slot, flip)
        deposit_if(u == 0, tile_0, mine_outer, slot, row, column)
        deposit_if(u == -1, tile_0, mine_inner, slot, row, column)
        deposit_if(u == 1, tile_1, mine_outer, slot, row, column)
        deposit_if(u == 0, tile_1, mine_inner, slot, row, column)
        u, row, column = box_meta(metas, 1, slot, flip)
        deposit_if(u == -1, tile_0, sib_inner, slot, row, column)
        deposit_if(u == 0, tile_1, sib_inner, slot, row, column)
        deposit_if(u == -1, tile_1, sib_outer, slot, row, column)


def inner_kernel(part, sib_outer, out_outer, beyond,
                 to_next, cross_0, cross_1, window_out, window_sib, tile, metas, sems):
    copy = pltpu.make_async_copy(part, tile, sems.at[3])
    copy.start()
    load_metas((sib_outer, out_outer, beyond), metas, sems)
    copy.wait()
    flip = lax.axis_index("dev") & 1
    for slot in range(2):
        u, row, column = box_meta(metas, 1, slot, flip)
        deposit_if(u == 1, tile, out_outer, slot, row, column)
        u, row, column = box_meta(metas, 2, slot, flip)
        deposit_if(u == -1, tile, beyond, slot, row, column)
    leaving = inbound(metas, 0, flip)
    _, row, column = box_meta(metas, 0, leaving, flip)
    extract(tile, (to_next,), row, column)
    _, row, column = box_meta(metas, 2, inbound(metas, 2, flip), flip)
    extract(tile, (cross_0, cross_1), row, column)
    _, row, column = box_meta(metas, 1, inbound(metas, 1, flip), flip)
    extract(tile, (window_out,), row, column)
    _, row, column = box_meta(metas, 0, 1 - leaving, flip)
    extract(tile, (window_sib,), row, column)


def outer_kernel(part, mine_outer, sib_outer, out_outer, out_inners,
                 to_next, sib_0, sib_1, window_out, window_sib, tile, metas, sems):
    copy = pltpu.make_async_copy(part, tile, sems.at[4])
    copy.start()
    load_metas((out_inners, out_outer, sib_outer, mine_outer), metas, sems, 2 * META + 1)
    copy.wait()
    flip = lax.axis_index("dev") & 1
    for slot in range(2):
        u, row, column = box_meta(metas, 1, slot, flip)
        deposit_if(u == 0, tile, out_outer, slot, row, column)
        deposit_if(u == 1, tile, out_inners, slot, row, column)
        u, row, column = box_meta(metas, 0, slot, flip)

        @pl.when(u == 1)
        def _(slot=slot, row=row, column=column):
            deposit(tile, out_inners, META + 1 + slot * HALF_BLOCKS, row, column)

    leaving = inbound(metas, 2, flip)
    _, row, column = box_meta(metas, 2, leaving, flip)
    extract(tile, (to_next,), row, column)
    _, row, column = box_meta(metas, 3, inbound(metas, 3, flip), flip)
    extract(tile, (sib_0, sib_1), row, column)
    _, row, column = box_meta(metas, 1, inbound(metas, 1, flip), flip)
    extract(tile, (window_out,), row, column)
    _, row, column = box_meta(metas, 2, 1 - leaving, flip)
    extract(tile, (window_sib,), row, column)


def neighbour_table():
    source = lax.broadcasted_iota(jnp.int32, (256, 128), 0) & 127
    target = lax.broadcasted_iota(jnp.int32, (256, 128), 1)
    beside = (jnp.abs(source - target) == 1) & ((source >> 6) == (target >> 6))
    return jnp.where(beside, 1.0, 0.0).astype(jnp.bfloat16)


def substep(source, factor, target, table):
    low = lax.broadcasted_iota(jnp.int32, (8, 128), 1) < 64
    parts = []
    for m in range(32):
        line = source[m + 1, 8:72]
        upper = line.astype(jnp.bfloat16)
        lower = (line - upper.astype(jnp.float32)).astype(jnp.bfloat16)
        parts.append(jnp.concatenate([upper, lower], axis=1))
    along = jnp.dot(jnp.concatenate(parts), table, preferred_element_type=jnp.float32)
    for m in range(32):
        for it in range(8):
            row = 8 + 8 * it
            value = source[m + 1, row:row + 8]
            beside = source[m + 1, row + 1:row + 9] + source[m + 1, row - 1:row + 7]
            lines = jnp.where(low, source[m + 2, row:row + 8], source[m, row:row + 8])
            beside += pltpu.roll(value + lines, 64, 1) + along[64 * m + 8 * it:64 * m + 8 * it + 8]
            rate = factor[m, 8 * it:8 * it + 8] - (time_step * quartic_rate) * (value * value)
            target[m + 1, row:row + 8] = value * rate + (time_step * gradient_energy) * beside


def relax_kernel(half_0, half_1, mine_outer, *refs, first, sizes):
    last = first < 0
    if last:
        held, result_hbm, factor, ping, pong, metas, sems = refs[-7:]
    else:
        ping, factor, pong, metas, sems = refs[-5:]
    windows, at = [], 0
    for size in sizes:
        windows.append(refs[at:at + size])
        at += size
    def edges():
        for buffer in (ping, pong):
            for at in (0, 33):
                buffer[at] = jnp.zeros(PADDED[1:], jnp.float32)
            for m in range(1, 33):
                buffer[m, 0:8] = jnp.zeros((8, 128), jnp.float32)
                buffer[m, 72:80] = jnp.zeros((8, 128), jnp.float32)

    load_metas((half_1, mine_outer), metas, sems, meanwhile=edges)
    flip = lax.axis_index("dev") & 1
    slot = inbound(metas, 0, flip) if first < 0 else 1 - inbound(metas, 0, flip)
    own_slot = inbound(metas, 1, flip)

    def results(box, to, sem):
        return [
            pltpu.make_async_copy(
                box.at[1:33, 8 + 8 * it:16 + 8 * it], result_hbm.at[to, it], sems.at[sem + it]
            )
            for it in range(8)
        ]

    copies = results(held, 1 - own_slot, 2) if last else []
    for copy in copies:
        copy.start()
    u, _, _ = box_meta(metas, 0, slot, flip)
    base = 1.0 + time_step * (growth_rate - 6.0 * gradient_energy)
    scale = 2.0 * coupling * time_step

    for g, half in ((0, half_0), (1, half_1)):
        at = jnp.where(flip == 1, 1 - g, g) * 32
        tile = first + u + g
        for index, window in enumerate(windows):
            @pl.when(tile == first - 1 + index)
            def _(window=window, half=half, at=at):
                def body(step, carry):
                    for sub in range(16):
                        m = step * 16 + sub
                        for it in range(4):
                            value = half[slot * HALF_BLOCKS + it * 32 + m]
                            rows = pl.multiple_of(at + 8 * it, 8)
                            ping[m + 1, pl.ds(pl.multiple_of(rows + 8, 8), 8)] = value
                            each = 4 // len(window)
                            others = window[it // each][it % each * 32 + m] - value * value
                            factor[m, pl.ds(rows, 8)] = base - scale * others
                    return carry

                lax.fori_loop(0, 2, body, 0)

    table = neighbour_table()

    def twice(step, carry):
        substep(ping, factor, pong, table)
        substep(pong, factor, ping, table)
        return carry

    lax.fori_loop(0, SUBSTEPS // 2, twice, 0)
    if last:
        mine = results(ping, own_slot, 10)
        for copy in mine:
            copy.start()
        for copy in copies + mine:
            copy.wait()


def on_device(grain_boxes, box_anchors, migrations):
    devices = lax.axis_size("dev")
    chips = devices // 2

    def pairs_of(even_step, odd_step):
        pairs = []
        for chip in range(chips):
            pairs.append((2 * chip, (2 * chip + even_step) % devices))
            pairs.append((2 * chip + 1, (2 * chip + 1 + odd_step) % devices))
        return pairs

    sibling, outward = pairs_of(1, -1), pairs_of(-1, 1)
    inward = pairs_of(2, -2)

    def send(value, pairs):
        return lax.ppermute(value, "dev", pairs)

    boxes = grain_boxes.reshape(2, 8, 8, 32, 128).transpose(0, 1, 3, 2, 4)

    vmem = pl.BlockSpec(memory_space=pltpu.VMEM)
    anywhere = pl.BlockSpec(memory_space=pl.ANY)
    params = pltpu.CompilerParams(vmem_limit_bytes=12 << 20)
    message_type = jax.ShapeDtypeStruct((2 * HALF_BLOCKS + 1, 8, 128), jnp.float32)
    tile_type = jax.ShapeDtypeStruct(TILE, jnp.float32)
    part_type = jax.ShapeDtypeStruct((HALF_BLOCKS // 2, 8, 128), jnp.float32)
    piece_type = jax.ShapeDtypeStruct(PIECE, jnp.float32)

    def metas(count, sems):
        return [pltpu.SMEM((count, 8, 128), jnp.float32), pltpu.SemaphoreType.DMA((sems,))]

    outer, inner = pl.pallas_call(
        message_kernel,
        in_specs=[pl.BlockSpec(memory_space=pltpu.HBM)] * 3,
        out_specs=[vmem] * 2,
        out_shape=[message_type] * 2,
        scratch_shapes=[
            pltpu.SMEM((2, 3), jnp.int32),
            pltpu.SMEM((1, 2), jnp.int32),
            pltpu.SemaphoreType.DMA((18,)),
        ],
        compiler_params=params,
        name="messages",
    )(*(pltpu.with_memory_space_constraint(a, pltpu.HBM) for a in (boxes, box_anchors, migrations)))

    out_outer = send(outer, outward)
    sib_outer = send(outer, sibling)
    sib_inner = send(inner, sibling)
    out_inners = send(jnp.concatenate([inner, sib_inner]), outward)

    part_0, part_1 = pl.pallas_call(
        local_kernel,
        in_specs=[vmem] * 4,
        out_specs=[vmem] * 2,
        out_shape=[tile_type] * 2,
        scratch_shapes=metas(2, 2),
        compiler_params=params,
        name="local_tiles",
    )(outer, inner, sib_outer, sib_inner)

    out_outer, part_1 = lax.optimization_barrier((out_outer, part_1))
    beyond = send(out_outer, sibling)

    tile_scratch = [pltpu.VMEM(TILE, jnp.float32)]
    to_next, cross_0, cross_1, window_out_1, window_sib_1 = pl.pallas_call(
        inner_kernel,
        in_specs=[anywhere] + [vmem] * 3,
        out_specs=[vmem] * 5,
        out_shape=[piece_type] + [part_type] * 2 + [piece_type] * 2,
        scratch_shapes=tile_scratch + metas(3, 4),
        compiler_params=params,
        name="inner_tile",
    )(part_1, sib_outer, out_outer, beyond)
    cross = [send(value, inward) for value in (cross_0, cross_1)]
    to_next, out_inners = lax.optimization_barrier((to_next, out_inners))
    near_out = send(to_next, inward)

    part_0, window_out_1 = lax.optimization_barrier((part_0, window_out_1))
    to_next, to_sib_0, to_sib_1, window_out_0, window_sib_0 = pl.pallas_call(
        outer_kernel,
        in_specs=[anywhere] + [vmem] * 4,
        out_specs=[vmem] * 5,
        out_shape=[piece_type] + [part_type] * 2 + [piece_type] * 2,
        scratch_shapes=tile_scratch + metas(4, 5),
        compiler_params=params,
        name="outer_tile",
    )(part_0, outer, sib_outer, out_outer, out_inners)
    far_out = send(to_next, inward)
    from_sib = [send(value, sibling) for value in (to_sib_0, to_sib_1)]
    *cross, near_out, window_out_0 = lax.optimization_barrier((*cross, near_out, window_out_0))
    near_sib = [send(value, sibling) for value in cross]

    def relax(name, first, halves, windows, held):
        flat = [value for window in windows for value in window] + held
        padded = [pltpu.VMEM(PADDED, jnp.float32)] * (1 + len(held))
        last_type = jax.ShapeDtypeStruct((2,) + BOX_BLOCKS, jnp.float32)
        return pl.pallas_call(
            functools.partial(relax_kernel, first=first, sizes=[len(w) for w in windows]),
            in_specs=[vmem] * (3 + len(flat)),
            out_specs=anywhere if held else vmem,
            out_shape=last_type if held else jax.ShapeDtypeStruct(PADDED, jnp.float32),
            scratch_shapes=[pltpu.VMEM((32, 64, 128), jnp.float32)] + padded + metas(2, 18),
            compiler_params=params,
            name=name,
        )(*halves, outer, *flat)

    held = relax(
        "relax_sibling", 1, (sib_inner, sib_outer),
        ([window_sib_0], [window_sib_1], from_sib, near_sib), [],
    )
    relaxed = relax(
        "relax_outer", -1, (out_inners, out_outer),
        ([far_out], [near_out], [window_out_0], [window_out_1]), [held],
    )
    return relaxed.transpose(0, 1, 3, 2, 4).reshape(grain_boxes.shape)


def solution(mesh):
    in_specs = (P("dev", None, None), P("dev", None), P("dev", None))
    out_specs = P("dev", None, None)
    return jax.shard_map(
        on_device, mesh=mesh, in_specs=in_specs, out_specs=out_specs, check_vma=False
    )
```

```python
import functools

import jax
import jax.numpy as jnp
from jax import lax
from jax.experimental import pallas as pl
from jax.experimental.pallas import tpu as pltpu
from jax.sharding import PartitionSpec as P

SUBSTEPS = 4

growth_rate = 1.0
quartic_rate = 1.0
coupling = 1.5
gradient_energy = 2.0
time_step = 0.02

HALF_BLOCKS = 128
PIECE = (HALF_BLOCKS, 8, 128)
TILE = (2, 64, 4, 8, 128)


META = 2 * HALF_BLOCKS
BOX_BLOCKS = (8, 32, 8, 128)
PADDED = (34, 80, 128)


def load_metas(refs, metas, sems, at=META, meanwhile=None):
    copies = [
        pltpu.make_async_copy(ref.at[META if n else at], metas.at[n], sems.at[n]) for n, ref in enumerate(refs)
    ]
    for copy in copies:
        copy.start()
    if meanwhile is not None:
        meanwhile()
    for copy in copies:
        copy.wait()


def number(metas, who, index):
    return metas[who, 0, index].astype(jnp.int32)


def box_meta(metas, who, slot, flip):
    first = slot == 0
    offset = jnp.where(first, number(metas, who, 0), number(metas, who, 1))
    row = jnp.where(first, number(metas, who, 2), number(metas, who, 3)) & 3
    column = jnp.where(first, number(metas, who, 4), number(metas, who, 5)) & 3
    return jnp.where(flip == 1, -offset, offset), row, column


def inbound(metas, who, flip):
    return jnp.where(flip == 1, number(metas, who, 7), number(metas, who, 6)) & 1


def deposit(tile_ref, piece_ref, base, row, column):
    lane = lax.broadcasted_iota(jnp.int32, (8, 128), 1)
    inside = ((lane - 32 * column) & 127) < 64
    shift = 32 * column
    shift_odd = (32 * column + 64) & 127

    def body(step, carry):
        for sub in range(16):
            m = step * 16 + sub
            place = (16 * row + m) & 63
            for it in range(4):
                value = piece_ref[base + it * 32 + m]
                value = value * value
                even = jnp.where(inside, pltpu.roll(value, shift, 1), 0.0)
                odd = jnp.where(inside, pltpu.roll(value, shift_odd, 1), 0.0)
                tile_ref[0, place, it] += even
                tile_ref[1, place, it] += odd
        return carry

    lax.fori_loop(0, 2, body, 0)


def extract(tile_ref, out_refs, row, column):
    lane = lax.broadcasted_iota(jnp.int32, (8, 128), 1)
    low = lane < 64
    shift = (128 - 32 * column) & 127
    shift_odd = (192 - 32 * column) & 127

    def body(step, carry):
        for sub in range(16):
            m = step * 16 + sub
            place = (16 * row + m) & 63
            for it in range(4):
                even = pltpu.roll(tile_ref[0, place, it], shift, 1)
                odd = pltpu.roll(tile_ref[1, place, it], shift_odd, 1)
                each = 4 // len(out_refs)
                out_refs[it // each][it % each * 32 + m] = jnp.where(low, even, odd)
        return carry

    lax.fori_loop(0, 2, body, 0)


def deposit_if(cond, tile_ref, piece_ref, slot, row, column):
    @pl.when(cond)
    def _():
        deposit(tile_ref, piece_ref, slot * HALF_BLOCKS, row, column)


def clear(tile_ref):
    def body(step, carry):
        for sub in range(4):
            for par in range(2):
                for it in range(4):
                    tile_ref[par, step * 4 + sub, it] = jnp.zeros((8, 128), jnp.float32)
        return carry

    lax.fori_loop(0, 16, body, 0)


def message_kernel(boxes, anchors_hbm, migrations_hbm, outer, inner, anchors, migrations, sem):
    position = lax.axis_index("dev")
    devices = lax.axis_size("dev")
    flip = position & 1
    small = [
        pltpu.make_async_copy(anchors_hbm, anchors, sem.at[16]),
        pltpu.make_async_copy(migrations_hbm, migrations, sem.at[17]),
    ]
    copies = []
    for message, first in ((outer, 4 * flip), (inner, 4 - 4 * flip)):
        for box in range(2):
            for it in range(4):
                at = pl.ds(box * HALF_BLOCKS + it * 32, 32)
                copies.append(
                    pltpu.make_async_copy(boxes.at[box, first + it], message.at[at], sem.at[len(copies)])
                )
    for copy in small + copies:
        copy.start()
    for copy in small:
        copy.wait()
    lane = lax.broadcasted_iota(jnp.int32, (8, 128), 1)
    values = []
    for box in range(2):
        ahead = anchors[box, 0] - position + 1
        ahead = jnp.where(ahead < 0, ahead + devices, ahead)
        values.append(jnp.where(ahead >= devices, ahead - devices, ahead) - 1)
    values += [anchors[box, axis] for axis in (1, 2) for box in range(2)]
    values += [migrations[0, 0], migrations[0, 1]]
    block = jnp.zeros((8, 128), jnp.int32)
    for index, value in enumerate(values):
        block = jnp.where(lane == index, value, block)
    block = block.astype(jnp.float32)
    outer[META] = block
    inner[META] = block
    for copy in copies:
        copy.wait()


def local_kernel(mine_outer, mine_inner, sib_outer, sib_inner, tile_0, tile_1, metas, sems):
    load_metas((mine_outer, sib_outer), metas, sems)
    flip = lax.axis_index("dev") & 1
    clear(tile_0)
    clear(tile_1)
    for slot in range(2):
        u, row, column = box_meta(metas, 0, slot, flip)
        deposit_if(u == 0, tile_0, mine_outer, slot, row, column)
        deposit_if(u == -1, tile_0, mine_inner, slot, row, column)
        deposit_if(u == 1, tile_1, mine_outer, slot, row, column)
        deposit_if(u == 0, tile_1, mine_inner, slot, row, column)
        u, row, column = box_meta(metas, 1, slot, flip)
        deposit_if(u == -1, tile_0, sib_inner, slot, row, column)
        deposit_if(u == 0, tile_1, sib_inner, slot, row, column)
        deposit_if(u == -1, tile_1, sib_outer, slot, row, column)


def inner_kernel(part, sib_outer, out_outer, beyond,
                 to_next, cross_0, cross_1, window_out, window_sib, tile, metas, sems):
    copy = pltpu.make_async_copy(part, tile, sems.at[3])
    copy.start()
    load_metas((sib_outer, out_outer, beyond), metas, sems)
    copy.wait()
    flip = lax.axis_index("dev") & 1
    for slot in range(2):
        u, row, column = box_meta(metas, 1, slot, flip)
        deposit_if(u == 1, tile, out_outer, slot, row, column)
        u, row, column = box_meta(metas, 2, slot, flip)
        deposit_if(u == -1, tile, beyond, slot, row, column)
    leaving = inbound(metas, 0, flip)
    _, row, column = box_meta(metas, 0, leaving, flip)
    extract(tile, (to_next,), row, column)
    _, row, column = box_meta(metas, 2, inbound(metas, 2, flip), flip)
    extract(tile, (cross_0, cross_1), row, column)
    _, row, column = box_meta(metas, 1, inbound(metas, 1, flip), flip)
    extract(tile, (window_out,), row, column)
    _, row, column = box_meta(metas, 0, 1 - leaving, flip)
    extract(tile, (window_sib,), row, column)


def outer_kernel(part, mine_outer, sib_outer, out_outer, out_inners,
                 to_next, sib_0, sib_1, window_out, window_sib, tile, metas, sems):
    copy = pltpu.make_async_copy(part, tile, sems.at[4])
    copy.start()
    load_metas((out_inners, out_outer, sib_outer, mine_outer), metas, sems, 2 * META + 1)
    copy.wait()
    flip = lax.axis_index("dev") & 1
    for slot in range(2):
        u, row, column = box_meta(metas, 1, slot, flip)
        deposit_if(u == 0, tile, out_outer, slot, row, column)
        deposit_if(u == 1, tile, out_inners, slot, row, column)
        u, row, column = box_meta(metas, 0, slot, flip)

        @pl.when(u == 1)
        def _(slot=slot, row=row, column=column):
            deposit(tile, out_inners, META + 1 + slot * HALF_BLOCKS, row, column)

    leaving = inbound(metas, 2, flip)
    _, row, column = box_meta(metas, 2, leaving, flip)
    extract(tile, (to_next,), row, column)
    _, row, column = box_meta(metas, 3, inbound(metas, 3, flip), flip)
    extract(tile, (sib_0, sib_1), row, column)
    _, row, column = box_meta(metas, 1, inbound(metas, 1, flip), flip)
    extract(tile, (window_out,), row, column)
    _, row, column = box_meta(metas, 2, 1 - leaving, flip)
    extract(tile, (window_sib,), row, column)


def neighbour_table():
    source = lax.broadcasted_iota(jnp.int32, (256, 128), 0) & 127
    target = lax.broadcasted_iota(jnp.int32, (256, 128), 1)
    beside = (jnp.abs(source - target) == 1) & ((source >> 6) == (target >> 6))
    return jnp.where(beside, 1.0, 0.0).astype(jnp.bfloat16)


def substep(source, factor, target, table):
    low = lax.broadcasted_iota(jnp.int32, (8, 128), 1) < 64
    parts = []
    for m in range(32):
        line = source[m + 1, 8:72]
        upper = line.astype(jnp.bfloat16)
        lower = (line - upper.astype(jnp.float32)).astype(jnp.bfloat16)
        parts.append(jnp.concatenate([upper, lower], axis=1))
    along = jnp.dot(jnp.concatenate(parts), table, preferred_element_type=jnp.float32)
    for m in range(32):
        for it in range(8):
            row = 8 + 8 * it
            value = source[m + 1, row:row + 8]
            beside = source[m + 1, row + 1:row + 9] + source[m + 1, row - 1:row + 7]
            lines = jnp.where(low, source[m + 2, row:row + 8], source[m, row:row + 8])
            beside += pltpu.roll(value + lines, 64, 1) + along[64 * m + 8 * it:64 * m + 8 * it + 8]
            rate = factor[m, 8 * it:8 * it + 8] - (time_step * quartic_rate) * (value * value)
            target[m + 1, row:row + 8] = value * rate + (time_step * gradient_energy) * beside


def relax_kernel(half_0, half_1, mine_outer, *refs, first, sizes):
    last = first < 0
    if last:
        held, result_hbm, factor, ping, pong, metas, sems = refs[-7:]
    else:
        ping, factor, pong, metas, sems = refs[-5:]
    windows, at = [], 0
    for size in sizes:
        windows.append(refs[at:at + size])
        at += size
    def edges():
        for buffer in (ping, pong):
            for at in (0, 33):
                buffer[at] = jnp.zeros(PADDED[1:], jnp.float32)
            for m in range(1, 33):
                buffer[m, 0:8] = jnp.zeros((8, 128), jnp.float32)
                buffer[m, 72:80] = jnp.zeros((8, 128), jnp.float32)

    load_metas((half_1, mine_outer), metas, sems, meanwhile=edges)
    flip = lax.axis_index("dev") & 1
    slot = inbound(metas, 0, flip) if first < 0 else 1 - inbound(metas, 0, flip)
    own_slot = inbound(metas, 1, flip)

    def results(box, to, sem):
        return [
            pltpu.make_async_copy(
                box.at[1:33, 8 + 8 * it:16 + 8 * it], result_hbm.at[to, it], sems.at[sem + it]
            )
            for it in range(8)
        ]

    copies = results(held, 1 - own_slot, 2) if last else []
    for copy in copies:
        copy.start()
    u, _, _ = box_meta(metas, 0, slot, flip)
    base = 1.0 + time_step * (growth_rate - 6.0 * gradient_energy)
    scale = 2.0 * coupling * time_step

    for g, half in ((0, half_0), (1, half_1)):
        at = jnp.where(flip == 1, 1 - g, g) * 32
        tile = first + u + g
        for index, window in enumerate(windows):
            @pl.when(tile == first - 1 + index)
            def _(window=window, half=half, at=at):
                def body(step, carry):
                    for sub in range(16):
                        m = step * 16 + sub
                        for it in range(4):
                            value = half[slot * HALF_BLOCKS + it * 32 + m]
                            rows = pl.multiple_of(at + 8 * it, 8)
                            ping[m + 1, pl.ds(pl.multiple_of(rows + 8, 8), 8)] = value
                            each = 4 // len(window)
                            others = window[it // each][it % each * 32 + m] - value * value
                            factor[m, pl.ds(rows, 8)] = base - scale * others
                    return carry

                lax.fori_loop(0, 2, body, 0)

    table = neighbour_table()

    def twice(step, carry):
        substep(ping, factor, pong, table)
        substep(pong, factor, ping, table)
        return carry

    lax.fori_loop(0, SUBSTEPS // 2, twice, 0)
    if last:
        mine = results(ping, own_slot, 10)
        for copy in mine:
            copy.start()
        for copy in copies + mine:
            copy.wait()


def on_device(grain_boxes, box_anchors, migrations):
    devices = lax.axis_size("dev")
    chips = devices // 2

    def pairs_of(even_step, odd_step):
        pairs = []
        for chip in range(chips):
            pairs.append((2 * chip, (2 * chip + even_step) % devices))
            pairs.append((2 * chip + 1, (2 * chip + 1 + odd_step) % devices))
        return pairs

    sibling, outward = pairs_of(1, -1), pairs_of(-1, 1)
    inward = pairs_of(2, -2)

    def send(value, pairs):
        return lax.ppermute(value, "dev", pairs)

    boxes = grain_boxes.reshape(2, 8, 8, 32, 128).transpose(0, 1, 3, 2, 4)

    vmem = pl.BlockSpec(memory_space=pltpu.VMEM)
    anywhere = pl.BlockSpec(memory_space=pl.ANY)
    params = pltpu.CompilerParams(vmem_limit_bytes=12 << 20)
    message_type = jax.ShapeDtypeStruct((2 * HALF_BLOCKS + 1, 8, 128), jnp.float32)
    tile_type = jax.ShapeDtypeStruct(TILE, jnp.float32)
    part_type = jax.ShapeDtypeStruct((HALF_BLOCKS // 2, 8, 128), jnp.float32)
    piece_type = jax.ShapeDtypeStruct(PIECE, jnp.float32)

    def metas(count, sems):
        return [pltpu.SMEM((count, 8, 128), jnp.float32), pltpu.SemaphoreType.DMA((sems,))]

    outer, inner = pl.pallas_call(
        message_kernel,
        in_specs=[pl.BlockSpec(memory_space=pltpu.HBM)] * 3,
        out_specs=[vmem] * 2,
        out_shape=[message_type] * 2,
        scratch_shapes=[
            pltpu.SMEM((2, 3), jnp.int32),
            pltpu.SMEM((1, 2), jnp.int32),
            pltpu.SemaphoreType.DMA((18,)),
        ],
        compiler_params=params,
        name="messages",
    )(*(pltpu.with_memory_space_constraint(a, pltpu.HBM) for a in (boxes, box_anchors, migrations)))

    out_outer = send(outer, outward)
    sib_outer = send(outer, sibling)
    sib_inner = send(inner, sibling)
    out_inners = send(jnp.concatenate([inner, sib_inner]), outward)

    part_0, part_1 = pl.pallas_call(
        local_kernel,
        in_specs=[vmem] * 4,
        out_specs=[vmem] * 2,
        out_shape=[tile_type] * 2,
        scratch_shapes=metas(2, 2),
        compiler_params=params,
        name="local_tiles",
    )(outer, inner, sib_outer, sib_inner)

    out_outer, part_1 = lax.optimization_barrier((out_outer, part_1))
    beyond = send(out_outer, sibling)

    tile_scratch = [pltpu.VMEM(TILE, jnp.float32)]
    to_next, cross_0, cross_1, window_out_1, window_sib_1 = pl.pallas_call(
        inner_kernel,
        in_specs=[anywhere] + [vmem] * 3,
        out_specs=[vmem] * 5,
        out_shape=[piece_type] + [part_type] * 2 + [piece_type] * 2,
        scratch_shapes=tile_scratch + metas(3, 4),
        compiler_params=params,
        name="inner_tile",
    )(part_1, sib_outer, out_outer, beyond)
    cross = [send(value, inward) for value in (cross_0, cross_1)]
    near_out = send(to_next, inward)

    part_0, window_out_1 = lax.optimization_barrier((part_0, window_out_1))
    to_next, to_sib_0, to_sib_1, window_out_0, window_sib_0 = pl.pallas_call(
        outer_kernel,
        in_specs=[anywhere] + [vmem] * 4,
        out_specs=[vmem] * 5,
        out_shape=[piece_type] + [part_type] * 2 + [piece_type] * 2,
        scratch_shapes=tile_scratch + metas(4, 5),
        compiler_params=params,
        name="outer_tile",
    )(part_0, outer, sib_outer, out_outer, out_inners)
    far_out = send(to_next, inward)
    from_sib = [send(value, sibling) for value in (to_sib_0, to_sib_1)]
    *cross, near_out, window_out_0 = lax.optimization_barrier((*cross, near_out, window_out_0))
    near_sib = [send(value, sibling) for value in cross]

    def relax(name, first, halves, windows, held):
        flat = [value for window in windows for value in window] + held
        padded = [pltpu.VMEM(PADDED, jnp.float32)] * (1 + len(held))
        last_type = jax.ShapeDtypeStruct((2,) + BOX_BLOCKS, jnp.float32)
        return pl.pallas_call(
            functools.partial(relax_kernel, first=first, sizes=[len(w) for w in windows]),
            in_specs=[vmem] * (3 + len(flat)),
            out_specs=anywhere if held else vmem,
            out_shape=last_type if held else jax.ShapeDtypeStruct(PADDED, jnp.float32),
            scratch_shapes=[pltpu.VMEM((32, 64, 128), jnp.float32)] + padded + metas(2, 18),
            compiler_params=params,
            name=name,
        )(*halves, outer, *flat)

    held = relax(
        "relax_sibling", 1, (sib_inner, sib_outer),
        ([window_sib_0], [window_sib_1], from_sib, near_sib), [],
    )
    relaxed = relax(
        "relax_outer", -1, (out_inners, out_outer),
        ([far_out], [near_out], [window_out_0], [window_out_1]), [held],
    )
    return relaxed.transpose(0, 1, 3, 2, 4).reshape(grain_boxes.shape)


def solution(mesh):
    in_specs = (P("dev", None, None), P("dev", None), P("dev", None))
    out_specs = P("dev", None, None)
    return jax.shard_map(
        on_device, mesh=mesh, in_specs=in_specs, out_specs=out_specs, check_vma=False
    )
```
